256 devices in a mesh: section: 8 (over x, core), fsdp: 8 (over z), seq: 4 (over y).
Axes of the slice: x: 4, y: 4, z: 8, core: 2. Of those that a mesh axis runs over, the one named last changes fastest.
Arguments:
- acts: bfloat16 [8, 8, 512, 1536], P('section', 'fsdp', 'seq')
- grad_out: bfloat16 [8, 512, 1536], P('fsdp', 'seq'), may hold values from -6 to 6
- gain: float32 [8, 1536], P('section'), may hold values from 0.5 to 2
- gate: float32 [8, 1536], P('section'), may hold values from 0.5 to 2
- w_query: bfloat16 [8, 1536, 1536], P('section', ('fsdp', 'seq'))
- kept: int32 [8, 8], P('fsdp'), may hold values from 0 to 1, as said below
- links: int32 [8, 4], P('fsdp', 'seq'), may hold values from 0 to 1, as said below
Outputs:
- grad_acts: bfloat16 [8, 8, 512, 1536], P('section', 'fsdp', 'seq')
- grad_wq: bfloat16 [8, 1536, 1536], P('section', ('fsdp', 'seq'))
The draws below stay inside these ranges and needn't reach their ends.
Inputs may be any that keep to these rules, and one draw needn't show every extreme that they name: `kept`: clip 0 runs every layer; the other entries vary. `links`: in clip 0 every tile after the first attends the tile before it; the other entries vary.
All inputs are finite; a program needn't handle non-finite values.
Results may differ from the reference program's by a relative error of at most 0.025.
The reference program's roundings to bfloat16 on the way count: a program that leaves them out, or rounds other values in their place, can miss the bound.
Values may be sent and summed in bfloat16 or wider, within the bound.
A program may use at most 64 MiB of HBM per device.

```python
import math
import jax
import jax.numpy as jnp
from jax import lax

D = 1536
HDIM = 128
TILE = 128
HEADS = 12
LAYERS = 8
CLIPS = 8
TILES = 4
TOKC = 512


def draw_acts(key, part):
    key_main = jax.random.fold_in(key, 0)
    full_shape = (LAYERS, CLIPS, TOKC, D)
    values_drawn = jax.random.normal(key_main, full_shape, jnp.float32)
    return values_drawn.astype(jnp.bfloat16)


def draw_w_query(key, part):
    key_main = jax.random.fold_in(key, 0)
    matrix = jax.random.normal(key_main, (LAYERS, D, D), jnp.float32) * D ** (-0.5)
    return matrix.astype(jnp.bfloat16)


def draw_kept(key, part):
    drawn = (jax.random.randint(jax.random.fold_in(key, 11), (CLIPS, LAYERS), 0, 4) > 0).astype(jnp.int32)
    first_clip = (lax.broadcasted_iota(jnp.int32, (CLIPS, LAYERS), 0) == 0).astype(jnp.int32)
    return jnp.maximum(drawn, first_clip)


def draw_links(key, part):
    drawn = jax.random.randint(jax.random.fold_in(key, 23), (CLIPS, TILES), 0, 2)
    first_clip = (lax.broadcasted_iota(jnp.int32, (CLIPS, TILES), 0) == 0).astype(jnp.int32)
    return jnp.maximum(drawn, first_clip).astype(jnp.int32)


def shard_levels(stream_key, dims, cuts, low, largest):
    def one(position, shards_of):
        heights = jax.random.uniform(jax.random.fold_in(jax.random.fold_in(stream_key, 6), position), (shards_of,), jnp.float32, low / len(cuts), largest / len(cuts))
        return jnp.repeat(jnp.exp(heights), dims[position] // shards_of).reshape((-1,) + (1,) * (len(dims) - position - 1))

    factor_of = one(*cuts[0])
    for cut in cuts[1:]:
        factor_of = factor_of * one(*cut)
    return factor_of


def normal_values(stream_key, dims, deviation, reach, shards=(), held_as=jnp.bfloat16):
    result = jax.random.normal(stream_key, dims, jnp.float32) * deviation
    if len(shards) > 0:
        result = shard_levels(stream_key, dims, shards, -0.22, 0.18) * result
    return jnp.clip(result, min=-reach, max=reach).astype(held_as)


def setup_inputs(seed: int = 0) -> dict:
    arg_keys = jax.random.split(jax.random.key(seed), 8)
    return {
        "acts": draw_acts(jax.random.fold_in(arg_keys[7], 71), 0),
        "grad_out": normal_values(arg_keys[1], (CLIPS, TOKC, D), 1.0, 6.0, ((0, 8), (1, 4))),
        "gain": jnp.clip(jnp.exp(math.log(2.0) - 1.3862944 * jax.random.uniform(arg_keys[2], (LAYERS, D), jnp.float32) ** shard_levels(arg_keys[2], (LAYERS, D), ((0, 8),), -0.2, 0.2)), 0.5, 2.0),
        "gate": jnp.clip(jnp.exp(math.log(2.0) - 1.3862944 * jax.random.uniform(arg_keys[3], (LAYERS, D), jnp.float32) ** shard_levels(arg_keys[3], (LAYERS, D), ((0, 8),), -0.2, 0.2)), 0.5, 2.0),
        "w_query": draw_w_query(jax.random.fold_in(arg_keys[7], 71), 0),
        "kept": draw_kept(jax.random.fold_in(arg_keys[7], 71), 0),
        "links": draw_links(jax.random.fold_in(arg_keys[7], 71), 0),
    }


norm_eps = 1e-06

def clip_backward(x_clip, dy_clip, keep_flag, links, gain_row, gate_row, weights):
    tile_count = TILES
    x_rows = x_clip.astype(jnp.float32).reshape(tile_count, TILE, D)
    inv_rms = lax.rsqrt(lax.optimization_barrier(jnp.mean(x_rows * x_rows, axis=-1, keepdims=True)) + norm_eps)
    normed = (x_rows * inv_rms * gain_row).astype(jnp.bfloat16)
    query_rows = jnp.dot(normed.reshape(tile_count * TILE, D), weights, preferred_element_type=jnp.float32)
    query_rows = query_rows.astype(jnp.bfloat16).reshape(tile_count, TILE, D)
    left_normed = jnp.concatenate([jnp.zeros_like(normed[:1]), normed[:-1]], axis=0)
    key_rows = jnp.concatenate([left_normed, normed], axis=1)
    positions = jnp.arange(tile_count, dtype=jnp.int32)
    linked = links * (positions > 0).astype(jnp.int32) > 0
    key_valid = jnp.concatenate([jnp.broadcast_to(linked[:, None], (tile_count, TILE)), jnp.ones((tile_count, TILE), dtype=jnp.bool_)], axis=1)
    score_scale = HDIM ** (-0.5)
    query_heads = query_rows.reshape(tile_count, TILE, HEADS, HDIM).astype(jnp.float32)
    key_heads = key_rows.reshape(tile_count, 2 * TILE, HEADS, HDIM).astype(jnp.float32)
    dy_tiles = dy_clip.reshape(tile_count, TILE, D)
    dy_float = dy_tiles.astype(jnp.float32)
    out_grad = (gate_row * dy_float).astype(jnp.bfloat16)
    grad_heads = out_grad.reshape(tile_count, TILE, HEADS, HDIM).astype(jnp.float32)
    scores = jnp.einsum('tihd,tjhd->thij', query_heads, key_heads) * score_scale
    scores = jnp.where(key_valid[:, None, None, :], scores, -1e+30)
    row_max = lax.optimization_barrier(jnp.max(scores, axis=-1, keepdims=True))
    exp_scores = jnp.exp(scores - row_max)
    prob_rows = exp_scores / lax.optimization_barrier(jnp.sum(exp_scores, axis=-1, keepdims=True))
    probs_low = lax.optimization_barrier(prob_rows.astype(jnp.bfloat16)).astype(jnp.float32)
    prob_grad = jnp.einsum('tihd,tjhd->thij', grad_heads, key_heads)
    row_delta = lax.optimization_barrier(jnp.sum(prob_rows * prob_grad, axis=-1, keepdims=True))
    score_grad = lax.optimization_barrier((prob_rows * (prob_grad - row_delta) * score_scale).astype(jnp.bfloat16)).astype(jnp.float32)
    query_grad = jnp.einsum('thij,tjhd->tihd', score_grad, key_heads).astype(jnp.bfloat16).reshape(tile_count, TILE, D)
    key_grad = jnp.einsum('thij,tihd->tjhd', score_grad, query_heads) + jnp.einsum('thij,tihd->tjhd', probs_low, grad_heads)
    key_grad = key_grad.reshape(tile_count, 2 * TILE, D)
    left_return = lax.optimization_barrier(key_grad[:, :TILE].astype(jnp.bfloat16)).astype(jnp.float32)
    from_right = jnp.concatenate([left_return[1:], jnp.zeros_like(left_return[:1])], axis=0)
    normed_grad = jnp.dot(query_grad.reshape(tile_count * TILE, D), weights.T, preferred_element_type=jnp.float32).reshape(tile_count, TILE, D)
    normed_grad = normed_grad + key_grad[:, TILE:] + from_right
    scaled_grad = normed_grad * gain_row
    mean_term = lax.optimization_barrier(jnp.mean(x_rows * scaled_grad, axis=-1, keepdims=True))
    change = inv_rms * (scaled_grad - x_rows * inv_rms * inv_rms * mean_term)
    updated = jnp.where(keep_flag > 0, (dy_float + change).astype(jnp.bfloat16), dy_tiles)
    tile_terms = jnp.einsum('tia,tib->tab', normed.astype(jnp.float32), query_grad.astype(jnp.float32))
    tile_terms = lax.optimization_barrier(tile_terms.astype(jnp.bfloat16)).astype(jnp.float32)
    weight_term = jnp.where(keep_flag > 0, lax.optimization_barrier(jnp.sum(tile_terms, axis=0)), jnp.zeros((D, D), jnp.float32))
    return (updated.reshape(tile_count * TILE, D), weight_term)

def reference(acts, grad_out, gain, gate, w_query, kept, links):
    dy_all = grad_out
    grad_list = [None] * LAYERS
    weight_list = [None] * LAYERS
    for section_index in reversed(range(LAYERS)):

        def one_clip(operands, section_index=section_index):
            x_clip, dy_clip, keep_flag, link_row = operands
            return clip_backward(x_clip, dy_clip, keep_flag, link_row, gain[section_index], gate[section_index], w_query[section_index])
        updated, weight_terms = lax.map(one_clip, (acts[section_index], dy_all, kept[:, section_index], links))
        grad_list[section_index] = updated
        weight_list[section_index] = lax.optimization_barrier(jnp.sum(weight_terms, axis=0)).astype(jnp.bfloat16)
        dy_all = updated
    return (jnp.stack(grad_list, axis=0), jnp.stack(weight_list, axis=0))
```

```python
import functools
import jax
import jax.numpy as jnp
from jax import lax
from jax.experimental import pallas as pl
from jax.experimental.pallas import tpu as pltpu
from jax.sharding import PartitionSpec as P

HDIM = 128
GROUP = 256
norm_eps = 1e-06
MESH = pl.DeviceIdType.MESH
NN = (((1,), (0,)), ((), ()))
NT = (((1,), (1,)), ((), ()))


def mm(a, b, dims=NN):
    return lax.dot_general(a, b, dims, preferred_element_type=jnp.float32)


def chain_kernel(
    x_ref, go_ref, gain_ref, gate_ref, w_ref, kept_ref, links_ref,
    out_ref, qg_ref, normed_ref,
    keys, inv_s, q_s, pt_s, kt_s, dy_buf, lr_send, lr_recv, kgo_s, ng_s, qg_s,
    nsend, nrecv, lsend, lrecv, dsend, drecv,
):
    sections = lax.axis_size("section")
    tiles = lax.axis_size("seq")
    sec = lax.axis_index("section")
    seq = lax.axis_index("seq")
    fsdp = lax.axis_index("fsdp")
    rows, width = x_ref.shape
    heads = width // HDIM
    groups = width // GROUP
    per_group = GROUP // HDIM
    scale = HDIM ** (-0.5)

    barrier = pltpu.get_barrier_semaphore()
    for other in (
        (lax.rem(sec + 1, sections), fsdp, seq),
        (lax.rem(sec + sections - 1, sections), fsdp, seq),
        (sec, fsdp, lax.rem(seq + 1, tiles)),
        (sec, fsdp, lax.rem(seq + tiles - 1, tiles)),
    ):
        pl.semaphore_signal(barrier, inc=1, device_id=other, device_id_type=MESH)

    keep = kept_ref[0, sec]
    linked = links_ref[0, 0] * jnp.minimum(seq, 1)

    def norm_block(step, carry):
        at = pl.ds(pl.multiple_of(step * 16, 16), 16)
        x_rows = x_ref[at, :].astype(jnp.float32)
        inv = lax.rsqrt(jnp.mean(x_rows * x_rows, axis=-1, keepdims=True) + norm_eps)
        inv_s[at, :] = jnp.broadcast_to(inv, (16, 128))
        rounded = (x_rows * inv * gain_ref[...]).astype(jnp.bfloat16)
        normed_ref[at, :] = rounded
        keys[pl.ds(pl.multiple_of(rows + step * 16, 16), 16), :] = rounded
        return carry

    lax.fori_loop(0, rows // 16, norm_block, 0)

    @pl.when(seq == 0)
    def _():
        keys[0:rows, :] = jnp.zeros((rows, width), jnp.bfloat16)

    @pl.when(seq == tiles - 1)
    def _():
        lr_recv[...] = jnp.zeros_like(lr_recv)

    pl.semaphore_wait(barrier, 4)

    left_copy = pltpu.make_async_remote_copy(
        src_ref=keys.at[pl.ds(rows, rows), :],
        dst_ref=keys.at[pl.ds(0, rows), :],
        send_sem=nsend,
        recv_sem=nrecv,
        device_id=(sec, fsdp, lax.rem(seq + 1, tiles)),
        device_id_type=MESH,
    )

    @pl.when(seq < tiles - 1)
    def _():
        left_copy.start()

    def query_block(step, carry):
        at = pl.ds(pl.multiple_of(step * GROUP, GROUP), GROUP)
        q_s[:, at] = mm(normed_ref[...], w_ref[:, at]).astype(jnp.bfloat16)
        return carry

    lax.fori_loop(0, groups, query_block, 0)

    @pl.when(seq > 0)
    def _():
        left_copy.wait_recv()

    @pl.when(seq < tiles - 1)
    def _():
        left_copy.wait_send()

    def probs_block(head, carry):
        at = pl.ds(pl.multiple_of(head * HDIM, HDIM), HDIM)
        key_part = keys[:, at]
        scores = mm(key_part, q_s[:, at], NT) * scale
        position = lax.broadcasted_iota(jnp.int32, scores.shape, 0)
        valid = position + linked * rows >= rows
        scores = jnp.where(valid, scores, -1e30)
        top = jnp.max(scores, axis=0, keepdims=True)
        weight = jnp.exp(scores - top)
        pt_s[head] = weight / jnp.sum(weight, axis=0, keepdims=True)
        kt_s[head] = key_part.T
        return carry

    lax.fori_loop(0, heads, probs_block, 0)

    @pl.when(sec == sections - 1)
    def _():
        dy_buf[...] = go_ref[...]

    def dy_copy(group):
        at = pl.ds(group * GROUP, GROUP)
        return pltpu.make_async_remote_copy(
            src_ref=out_ref.at[:, at],
            dst_ref=dy_buf.at[:, at],
            send_sem=dsend.at[group],
            recv_sem=drecv.at[group],
            device_id=(lax.rem(sec + sections - 1, sections), fsdp, seq),
            device_id_type=MESH,
        )

    def lr_copy(group):
        at = pl.ds(group * GROUP, GROUP)
        return pltpu.make_async_remote_copy(
            src_ref=lr_send.at[:, at],
            dst_ref=lr_recv.at[:, at],
            send_sem=lsend.at[group],
            recv_sem=lrecv.at[group],
            device_id=(sec, fsdp, lax.rem(seq + tiles - 1, tiles)),
            device_id_type=MESH,
        )

    def attention(group):
        for head in range(group * per_group, (group + 1) * per_group):
            at = pl.ds(head * HDIM, HDIM)
            grad = (gate_ref[:, at] * dy_buf[:, at].astype(jnp.float32)).astype(jnp.bfloat16)
            probs = pt_s[head]
            prob_grad = mm(keys[:, at], grad, NT)
            delta = jnp.sum(probs * prob_grad, axis=0, keepdims=True)
            score_grad = (probs * (prob_grad - delta) * scale).astype(jnp.bfloat16)
            key_grad = mm(
                jnp.concatenate([score_grad, probs.astype(jnp.bfloat16)], axis=1),
                jnp.concatenate([q_s[:, at], grad], axis=0),
            )
            lr_send[:, at] = key_grad[:rows].astype(jnp.bfloat16)
            kgo_s[:, at] = key_grad[rows:]
            qg_s[:, at] = mm(kt_s[head], score_grad).astype(jnp.bfloat16).T

    def project(group):
        at = pl.ds(group * GROUP, GROUP)
        part = mm(qg_s[:, at], w_ref[:, at], NT)
        if group == 0:
            ng_s[...] = part
        else:
            ng_s[...] += part

    for group in range(groups):

        @pl.when(sec < sections - 1)
        def _():
            dy_copy(group).wait_recv()

        attention(group)

        @pl.when(seq > 0)
        def _():
            lr_copy(group).start()

        if group > 0:
            project(group - 1)
    project(groups - 1)

    @pl.when(seq < tiles - 1)
    def _():
        for group in range(groups):
            lr_copy(group).wait_recv()

    def finish_block(step, carry):
        at = pl.ds(pl.multiple_of(step * 16, 16), 16)
        x_rows = x_ref[at, :].astype(jnp.float32)
        inv = inv_s[at, 0:1]
        total = ng_s[at, :] + kgo_s[at, :] + lr_recv[at, :].astype(jnp.float32)
        total = total * gain_ref[...]
        mean_term = jnp.mean(x_rows * total, axis=-1, keepdims=True)
        change = inv * (total - x_rows * (inv * inv * mean_term))
        before = dy_buf[at, :].astype(jnp.float32)
        kept_here = jnp.full(before.shape, keep, jnp.int32) > 0
        out_ref[at, :] = jnp.where(kept_here, before + change, before).astype(jnp.bfloat16)
        return carry

    lax.fori_loop(0, rows // 16, finish_block, 0)

    @pl.when(sec > 0)
    def _():
        for group in range(groups):
            dy_copy(group).start()

    grads = qg_s[...].astype(jnp.float32)
    qg_ref[...] = jnp.where(
        jnp.full(grads.shape, keep, jnp.int32) > 0, grads, jnp.zeros_like(grads)
    ).astype(jnp.bfloat16)

    @pl.when(seq > 0)
    def _():
        for group in range(groups):
            lr_copy(group).wait_send()

    @pl.when(sec > 0)
    def _():
        for group in range(groups):
            dy_copy(group).wait_send()


def run_chain(x, grad_out, gain, gate, weights, kept, links):
    rows, width = x.shape
    heads = width // HDIM
    groups = width // GROUP
    vmem = pl.BlockSpec(memory_space=pltpu.VMEM)
    smem = pl.BlockSpec(memory_space=pltpu.SMEM)
    low = jnp.bfloat16
    block = jax.ShapeDtypeStruct((rows, width), low)
    return pl.pallas_call(
        chain_kernel,
        out_shape=(block, block, block),
        in_specs=[vmem] * 5 + [smem] * 2,
        out_specs=(vmem, vmem, vmem),
        scratch_shapes=[
            pltpu.VMEM((2 * rows, width), low),
            pltpu.VMEM((rows, 128), jnp.float32),
            pltpu.VMEM((rows, width), low),
            pltpu.VMEM((heads, 2 * rows, rows), jnp.float32),
            pltpu.VMEM((heads, HDIM, 2 * rows), low),
            pltpu.VMEM((rows, width), low),
            pltpu.VMEM((rows, width), low),
            pltpu.VMEM((rows, width), low),
            pltpu.VMEM((rows, width), jnp.float32),
            pltpu.VMEM((rows, width), jnp.float32),
            pltpu.VMEM((rows, width), low),
            pltpu.SemaphoreType.DMA,
            pltpu.SemaphoreType.DMA,
            pltpu.SemaphoreType.DMA((groups,)),
            pltpu.SemaphoreType.DMA((groups,)),
            pltpu.SemaphoreType.DMA((groups,)),
            pltpu.SemaphoreType.DMA((groups,)),
        ],
        compiler_params=pltpu.CompilerParams(
            collective_id=0, has_side_effects=True, vmem_limit_bytes=56 * 2**20
        ),
        name="chain",
    )(x, grad_out, gain, gate, weights, kept, links)


def per_device(acts, grad_out, gain, gate, w_query, kept, links):
    weights = lax.all_gather(w_query[0], ("fsdp", "seq"), axis=0, tiled=True)
    result, query_grad, normed = run_chain(
        acts[0, 0], grad_out[0], gain, gate, weights, kept, links
    )
    grad_rows = lax.psum_scatter(
        lax.dot_general(
            normed, query_grad, (((0,), (0,)), ((), ())), preferred_element_type=jnp.float32
        ).astype(jnp.bfloat16),
        ("fsdp", "seq"),
        scatter_dimension=0,
        tiled=True,
    )
    return (result[None, None], grad_rows[None])


def solution(mesh):
    placed = (
        P("section", "fsdp", "seq", None),
        P("fsdp", "seq", None),
        P("section", None),
        P("section", None),
        P("section", ("fsdp", "seq"), None),
        P("fsdp", None),
        P("fsdp", "seq"),
    )
    return jax.shard_map(
        per_device,
        mesh=mesh,
        in_specs=placed,
        out_specs=(P("section", "fsdp", "seq", None), P("section", ("fsdp", "seq"), None)),
        check_vma=False,
    )
```

```python
import jax
import jax.numpy as jnp
from jax import lax
from jax.experimental import pallas as pl
from jax.experimental.pallas import tpu as pltpu
from jax.sharding import PartitionSpec as P

HDIM = 128
GROUP = 256
norm_eps = 1e-06
MESH = pl.DeviceIdType.MESH
NN = (((1,), (0,)), ((), ()))
NT = (((1,), (1,)), ((), ()))


def mm(a, b, dims=NN):
    return lax.dot_general(a, b, dims, preferred_element_type=jnp.float32)


LINK_RATE = 85e3
HOP_TIME = 1.7
BLOCK_TIME = 0.6


def hops_of(size, flip):
    far, near = size // 2, size - 1 - size // 2
    return ((1, near), (-1, far)) if flip else ((1, far), (-1, near))


def spread_plan(size_z, size_y):
    plan = []
    sizes = (size_z, size_y)
    for part, first in ((1, 0), (0, 1)):
        second = 1 - first
        held = [(0, None)]
        for sign, hops in hops_of(sizes[first], False):
            before = None
            for hop in range(1, hops + 1):
                block = [0, 0]
                block[first] = -sign * (hop - 1)
                plan.append((first, sign, tuple(block), part, [] if before is None else [before]))
                before = len(plan) - 1
                held.append((-sign * hop, before))
        for stream, (offset, source) in enumerate(held):
            for sign, hops in hops_of(sizes[second], stream % 2 == 1):
                before = source
                for hop in range(1, hops + 1):
                    block = [0, 0]
                    block[first] = offset
                    block[second] = -sign * (hop - 1)
                    plan.append(
                        (second, sign, tuple(block), part, [] if before is None else [before])
                    )
                    before = len(plan) - 1
    return plan


def far_first(size):
    order = []
    for sign, hops in hops_of(size, False):
        order += [sign * hop for hop in range(1, hops + 1)]
    return sorted(order, key=lambda step: (-abs(step), -step)) + [0]


def sum_plan(size_z, size_y):
    plan, ends = [], {}
    sizes = (size_z, size_y)
    for part, first in ((0, 0), (1, 1)):
        second = 1 - first
        landed = {}
        for stream, offset in enumerate(far_first(sizes[second])):
            landed[offset % sizes[second]] = last = []
            for sign, hops in hops_of(sizes[first], stream % 2 == 1):
                for hop in range(1, hops + 1):
                    block = [0, 0]
                    block[second] = offset
                    block[first] = sign * (hops + 1 - hop)
                    plan.append(
                        (first, sign, tuple(block), part, [] if hop == 1 else [len(plan) - 1])
                    )
                if hops:
                    last.append(len(plan) - 1)
        last = list(landed[0])
        for sign, hops in hops_of(sizes[second], False):
            for hop in range(1, hops + 1):
                block = [0, 0]
                block[second] = sign * (hops + 1 - hop)
                adds = list(landed[block[second] % sizes[second]])
                plan.append(
                    (second, sign, tuple(block), part, adds + ([] if hop == 1 else [len(plan) - 1]))
                )
            if hops:
                last.append(len(plan) - 1)
        ends[part] = last
    return plan, ends


def run_plan(plan, part_bytes, ready):
    free, arrival, events = {}, {}, []
    done, started, now = set(), set(), 0.0
    made = set()
    todo = list(ready)

    def launch():
        for index, (axis, sign, block, part, deps) in enumerate(plan):
            if index in started or any(dep not in done for dep in deps):
                continue
            if ready and block[0] not in made:
                continue
            started.add(index)
            begin = max(now, free.get((axis, sign), 0.0))
            free[axis, sign] = begin + part_bytes[part] / LINK_RATE
            arrival[index] = free[axis, sign] + HOP_TIME
            events.append(("start", index))

    launch()
    while len(done) < len(plan):
        coming = sorted((when, index) for index, when in arrival.items() if index not in done)
        if todo and (not coming or coming[0][0] > now):
            step = todo.pop(0)
            events.append(("make", step))
            made.update(step)
            now += BLOCK_TIME
        else:
            when, index = coming[0]
            now = max(now, when)
            done.add(index)
            events.append(("wait", index))
        launch()
    return events


def chain_kernel(
    x_ref, go_ref, gain_ref, gate_ref, shard_ref, kept_ref, links_ref,
    out_ref, grad_ref,
    w_ref, wgrad, slots_a, slots_b,
    keys, inv_s, q_s, pt_s, kt_s, dy_buf, lr_send, lr_recv, kgo_s, ng_s, qg_s,
    own_sem, turn, gsend, grecv, ssend, srecv,
    nsend, nrecv, lsend, lrecv, dsend, drecv,
):
    sections = lax.axis_size("section")
    tiles = lax.axis_size("seq")
    sec = lax.axis_index("section")
    seq = lax.axis_index("seq")
    fsdp = lax.axis_index("fsdp")
    rows, width = x_ref.shape
    heads = width // HDIM
    groups = width // GROUP
    per_group = GROUP // HDIM
    scale = HDIM ** (-0.5)
    ring_z = lax.axis_size("fsdp")
    shard = width // (ring_z * tiles)
    cut = first_columns(width)
    columns = (pl.ds(0, cut), pl.ds(cut, width - cut))
    part_bytes = (2 * shard * cut, 2 * shard * (width - cut))

    def neighbour(axis, sign):
        if axis == 0:
            return (sec, lax.rem(fsdp + sign + ring_z, ring_z), seq)
        return (sec, fsdp, lax.rem(seq + sign + tiles, tiles))

    def rows_of(block):
        at_z = lax.rem(fsdp + block[0] + ring_z, ring_z)
        at_y = lax.rem(seq + block[1] + tiles, tiles)
        return pl.ds(pl.multiple_of((at_z * tiles + at_y) * shard, shard), shard)

    barrier = pltpu.get_barrier_semaphore()
    for other in (
        (lax.rem(sec + 1, sections), fsdp, seq),
        (lax.rem(sec + sections - 1, sections), fsdp, seq),
        (sec, fsdp, lax.rem(seq + 1, tiles)),
        (sec, fsdp, lax.rem(seq + tiles - 1, tiles)),
        (sec, lax.rem(fsdp + 1, ring_z), seq),
        (sec, lax.rem(fsdp + ring_z - 1, ring_z), seq),
    ):
        pl.semaphore_signal(barrier, inc=1, device_id=other, device_id_type=MESH)

    own_copy = pltpu.make_async_copy(shard_ref, w_ref.at[rows_of((0, 0)), :], own_sem)
    own_copy.start()
    keep = kept_ref[0, sec]
    linked = links_ref[0, 0] * jnp.minimum(seq, 1)

    def norm_block(step, carry):
        at = pl.ds(pl.multiple_of(step * 16, 16), 16)
        x_rows = x_ref[at, :].astype(jnp.float32)
        inv = lax.rsqrt(jnp.mean(x_rows * x_rows, axis=-1, keepdims=True) + norm_eps)
        inv_s[at, :] = jnp.broadcast_to(inv, (16, 128))
        rounded = (x_rows * inv * gain_ref[...]).astype(jnp.bfloat16)
        keys[pl.ds(pl.multiple_of(rows + step * 16, 16), 16), :] = rounded
        return carry

    lax.fori_loop(0, rows // 16, norm_block, 0)

    @pl.when(seq == 0)
    def _():
        keys[0:rows, :] = jnp.zeros((rows, width), jnp.bfloat16)

    @pl.when(seq == tiles - 1)
    def _():
        lr_recv[...] = jnp.zeros_like(lr_recv)

    pl.semaphore_wait(barrier, 6)
    own_copy.wait()

    left_copy = pltpu.make_async_remote_copy(
        src_ref=keys.at[pl.ds(rows, rows), :],
        dst_ref=keys.at[pl.ds(0, rows), :],
        send_sem=nsend,
        recv_sem=nrecv,
        device_id=(sec, fsdp, lax.rem(seq + 1, tiles)),
        device_id_type=MESH,
    )

    @pl.when(seq < tiles - 1)
    def _():
        left_copy.start()

    gather = spread_plan(ring_z, tiles)

    def gather_copy(index):
        axis, sign, block, part, _ = gather[index]
        place = w_ref.at[rows_of(block), columns[part]]
        return pltpu.make_async_remote_copy(
            src_ref=place,
            dst_ref=place,
            send_sem=gsend.at[index],
            recv_sem=grecv.at[index],
            device_id=neighbour(axis, sign),
            device_id_type=MESH,
        )

    if sections % 2 == 0:

        @pl.when(lax.rem(sec, 2) == 0)
        def _():
            pl.semaphore_wait(turn, 1)

    for kind, index in run_plan(gather, part_bytes, ()):
        if kind == "start":
            gather_copy(index).start()
        else:
            gather_copy(index).wait_recv()
    for index in range(len(gather)):
        gather_copy(index).wait_send()
    if sections % 2 == 0:

        @pl.when(lax.rem(sec, 2) == 1)
        def _():
            pl.semaphore_signal(
                turn, inc=1, device_id=(sec - 1, fsdp, seq), device_id_type=MESH
            )

    def query_block(step, carry):
        at = pl.ds(pl.multiple_of(step * GROUP, GROUP), GROUP)
        q_s[:, at] = mm(keys[rows:, :], w_ref[:, at]).astype(jnp.bfloat16)
        return carry

    lax.fori_loop(0, groups, query_block, 0)

    @pl.when(seq > 0)
    def _():
        left_copy.wait_recv()

    @pl.when(seq < tiles - 1)
    def _():
        left_copy.wait_send()

    def probs_block(head, carry):
        at = pl.ds(pl.multiple_of(head * HDIM, HDIM), HDIM)
        key_part = keys[:, at]
        scores = mm(key_part, q_s[:, at], NT) * scale
        position = lax.broadcasted_iota(jnp.int32, scores.shape, 0)
        valid = position + linked * rows >= rows
        scores = jnp.where(valid, scores, -1e30)
        top = jnp.max(scores, axis=0, keepdims=True)
        weight = jnp.exp(scores - top)
        pt_s[head] = weight / jnp.sum(weight, axis=0, keepdims=True)
        kt_s[at, :] = key_part.T
        return carry

    lax.fori_loop(0, heads, probs_block, 0)

    @pl.when(sec == sections - 1)
    def _():
        dy_buf[...] = go_ref[...]

    def dy_copy(group):
        at = pl.ds(group * GROUP, GROUP)
        return pltpu.make_async_remote_copy(
            src_ref=out_ref.at[:, at],
            dst_ref=dy_buf.at[:, at],
            send_sem=dsend.at[group],
            recv_sem=drecv.at[group],
            device_id=(lax.rem(sec + sections - 1, sections), fsdp, seq),
            device_id_type=MESH,
        )

    def lr_copy(group):
        at = pl.ds(group * GROUP, GROUP)
        return pltpu.make_async_remote_copy(
            src_ref=lr_send.at[:, at],
            dst_ref=lr_recv.at[:, at],
            send_sem=lsend.at[group],
            recv_sem=lrecv.at[group],
            device_id=(sec, fsdp, lax.rem(seq + tiles - 1, tiles)),
            device_id_type=MESH,
        )

    def attention(group):
        for head in range(group * per_group, (group + 1) * per_group):
            at = pl.ds(head * HDIM, HDIM)
            grad = (gate_ref[:, at] * dy_buf[:, at].astype(jnp.float32)).astype(jnp.bfloat16)
            probs = pt_s[head]
            prob_grad = mm(keys[:, at], grad, NT)
            delta = jnp.sum(probs * prob_grad, axis=0, keepdims=True)
            score_grad = (probs * (prob_grad - delta) * scale).astype(jnp.bfloat16)
            key_grad = mm(
                jnp.concatenate([score_grad, probs.astype(jnp.bfloat16)], axis=1),
                jnp.concatenate([q_s[:, at], grad], axis=0),
            )
            lr_send[:, at] = key_grad[:rows].astype(jnp.bfloat16)
            kgo_s[:, at] = key_grad[rows:]
            qg_s[:, at] = mm(kt_s[at, :], score_grad).astype(jnp.bfloat16).T

    def project(group):
        at = pl.ds(group * GROUP, GROUP)
        part = mm(qg_s[:, at], w_ref[:, at], NT)
        if group == 0:
            ng_s[...] = part
        else:
            ng_s[...] += part

    for group in range(groups):

        @pl.when(sec < sections - 1)
        def _():
            dy_copy(group).wait_recv()

        attention(group)

        @pl.when(seq > 0)
        def _():
            lr_copy(group).start()

        if group > 0:
            project(group - 1)
    project(groups - 1)

    @pl.when(seq < tiles - 1)
    def _():
        for group in range(groups):
            lr_copy(group).wait_recv()

    def finish_block(step, carry):
        at = pl.ds(pl.multiple_of(step * 16, 16), 16)
        x_rows = x_ref[at, :].astype(jnp.float32)
        inv = inv_s[at, 0:1]
        total = ng_s[at, :] + kgo_s[at, :] + lr_recv[at, :].astype(jnp.float32)
        total = total * gain_ref[...]
        mean_term = jnp.mean(x_rows * total, axis=-1, keepdims=True)
        change = inv * (total - x_rows * (inv * inv * mean_term))
        before = dy_buf[at, :].astype(jnp.float32)
        kept_here = jnp.full(before.shape, keep, jnp.int32) > 0
        out_ref[at, :] = jnp.where(kept_here, before + change, before).astype(jnp.bfloat16)
        return carry

    lax.fori_loop(0, rows // 16, finish_block, 0)

    @pl.when(sec > 0)
    def _():
        for group in range(groups):
            dy_copy(group).start()

    grads = qg_s[...].astype(jnp.float32)
    qg_s[...] = jnp.where(
        jnp.full(grads.shape, keep, jnp.int32) > 0, grads, jnp.zeros_like(grads)
    ).astype(jnp.bfloat16)

    sums, ends = sum_plan(ring_z, tiles)
    slot_refs = (slots_a, slots_b)
    slot_at, used = {}, [0, 0]
    for index, (_, _, _, part, _) in enumerate(sums):
        slot_at[index] = used[part]
        used[part] += 1

    def sum_copy(index):
        axis, sign, block, part, _ = sums[index]
        return pltpu.make_async_remote_copy(
            src_ref=wgrad.at[rows_of(block), columns[part]],
            dst_ref=slot_refs[part].at[slot_at[index]],
            send_sem=ssend.at[index],
            recv_sem=srecv.at[index],
            device_id=neighbour(axis, sign),
            device_id_type=MESH,
        )

    def summed(block, part, adds):
        total = wgrad[rows_of(block), columns[part]].astype(jnp.float32)
        for index in adds:
            total = total + slot_refs[part][slot_at[index]].astype(jnp.float32)
        return total.astype(jnp.bfloat16)

    def make(offset):
        span = tiles * shard
        start = lax.rem(fsdp + offset + ring_z, ring_z) * span
        at = pl.ds(pl.multiple_of(start, shard), span)
        left = kt_s[at, rows : 2 * rows]
        for group in range(groups):
            to = pl.ds(group * GROUP, GROUP)
            wgrad[at, to] = mm(left, qg_s[:, to]).astype(jnp.bfloat16)

    makes = []
    for offset in far_first(ring_z):
        makes.append((offset, offset - ring_z, offset + ring_z))
    for kind, index in run_plan(sums, part_bytes, makes):
        if kind == "make":
            make(index[0])
        elif kind == "start":
            _, _, block, part, adds = sums[index]
            if adds:
                wgrad[rows_of(block), columns[part]] = summed(block, part, adds)
            sum_copy(index).start()
        else:
            sum_copy(index).wait_recv()
    for part in (0, 1):
        grad_ref[:, columns[part]] = summed((0, 0), part, ends[part])
    for index in range(len(sums)):
        sum_copy(index).wait_send()

    @pl.when(seq > 0)
    def _():
        for group in range(groups):
            lr_copy(group).wait_send()

    @pl.when(sec > 0)
    def _():
        for group in range(groups):
            dy_copy(group).wait_send()


def first_columns(width):
    return max(1, round(width * 5 / 12 / 128)) * 128


def run_chain(x, grad_out, gain, gate, shard, kept, links):
    rows, width = x.shape
    heads = width // HDIM
    groups = width // GROUP
    vmem = pl.BlockSpec(memory_space=pltpu.VMEM)
    smem = pl.BlockSpec(memory_space=pltpu.SMEM)
    low = jnp.bfloat16
    count = lax.axis_size("fsdp") * lax.axis_size("seq") - 1
    cut = first_columns(width)
    dma = pltpu.SemaphoreType.DMA
    return pl.pallas_call(
        chain_kernel,
        out_shape=(
            jax.ShapeDtypeStruct((rows, width), low),
            jax.ShapeDtypeStruct(shard.shape, low),
        ),
        in_specs=[vmem] * 5 + [smem] * 2,
        out_specs=(vmem, vmem),
        scratch_shapes=[
            pltpu.VMEM((width, width), low),
            pltpu.VMEM((width, width), low),
            pltpu.VMEM((count, shard.shape[0], cut), low),
            pltpu.VMEM((count, shard.shape[0], width - cut), low),
            pltpu.VMEM((2 * rows, width), low),
            pltpu.VMEM((rows, 128), jnp.float32),
            pltpu.VMEM((rows, width), low),
            pltpu.VMEM((heads, 2 * rows, rows), jnp.float32),
            pltpu.VMEM((width, 2 * rows), low),
            pltpu.VMEM((rows, width), low),
            pltpu.VMEM((rows, width), low),
            pltpu.VMEM((rows, width), low),
            pltpu.VMEM((rows, width), jnp.float32),
            pltpu.VMEM((rows, width), jnp.float32),
            pltpu.VMEM((rows, width), low),
            dma,
            pltpu.SemaphoreType.REGULAR,
            dma((2 * count,)),
            dma((2 * count,)),
            dma((2 * count,)),
            dma((2 * count,)),
            dma,
            dma,
            dma((groups,)),
            dma((groups,)),
            dma((groups,)),
            dma((groups,)),
        ],
        compiler_params=pltpu.CompilerParams(
            collective_id=0, has_side_effects=True, vmem_limit_bytes=56 * 2**20
        ),
        name="chain",
    )(x, grad_out, gain, gate, shard, kept, links)


def per_device(acts, grad_out, gain, gate, w_query, kept, links):
    result, grad_rows = run_chain(
        acts[0, 0], grad_out[0], gain, gate, w_query[0], kept, links
    )
    return (result[None, None], grad_rows[None])


def solution(mesh):
    placed = (
        P("section", "fsdp", "seq", None),
        P("fsdp", "seq", None),
        P("section", None),
        P("section", None),
        P("section", ("fsdp", "seq"), None),
        P("fsdp", None),
        P("fsdp", "seq"),
    )
    return jax.shard_map(
        per_device,
        mesh=mesh,
        in_specs=placed,
        out_specs=(P("section", "fsdp", "seq", None), P("section", ("fsdp", "seq"), None)),
        check_vma=False,
    )
```

```python
import jax
import jax.numpy as jnp
from jax import lax
from jax.experimental import pallas as pl
from jax.experimental.pallas import tpu as pltpu
from jax.sharding import PartitionSpec as P

HDIM = 128
GROUP = 256
norm_eps = 1e-06
MESH = pl.DeviceIdType.MESH
NN = (((1,), (0,)), ((), ()))
NT = (((1,), (1,)), ((), ()))


def mm(a, b, dims=NN):
    return lax.dot_general(a, b, dims, preferred_element_type=jnp.float32)


LINK_RATE = 85e3
HOP_TIME = 1.9
BLOCK_TIME = 0.5
BACKLOG = 0.6
LEFT_PARTS = 4


def hops_of(size, flip):
    far, near = size // 2, size - 1 - size // 2
    return ((1, near), (-1, far)) if flip else ((1, far), (-1, near))


def spread_plan(size_z, size_y):
    plan = []
    sizes = (size_z, size_y)
    for part, first in ((1, 0), (0, 1)):
        second = 1 - first
        held = [(0, None)]
        for sign, hops in hops_of(sizes[first], False):
            before = None
            for hop in range(1, hops + 1):
                block = [0, 0]
                block[first] = -sign * (hop - 1)
                plan.append((first, sign, tuple(block), part, [] if before is None else [before]))
                before = len(plan) - 1
                held.append((-sign * hop, before))
        for stream, (offset, source) in enumerate(held):
            flip = stream % 2 == 1 if second == 0 else stream % 4 != 0
            for sign, hops in hops_of(sizes[second], flip):
                before = source
                for hop in range(1, hops + 1):
                    block = [0, 0]
                    block[first] = offset
                    block[second] = -sign * (hop - 1)
                    plan.append(
                        (second, sign, tuple(block), part, [] if before is None else [before])
                    )
                    before = len(plan) - 1
    return plan


def far_first(size):
    order = []
    for sign, hops in hops_of(size, False):
        order += [sign * hop for hop in range(1, hops + 1)]
    return sorted(order, key=lambda step: (-abs(step), -step)) + [0]


def sum_plan(size_z, size_y):
    plan, ends = [], {}
    sizes = (size_z, size_y)
    for part, first in ((0, 0), (1, 1)):
        second = 1 - first
        landed = {}
        for stream, offset in enumerate(far_first(sizes[second])):
            landed[offset % sizes[second]] = last = []
            for sign, hops in hops_of(sizes[first], stream % 2 == 1):
                for hop in range(1, hops + 1):
                    block = [0, 0]
                    block[second] = offset
                    block[first] = sign * (hops + 1 - hop)
                    plan.append(
                        (first, sign, tuple(block), part, [] if hop == 1 else [len(plan) - 1])
                    )
                if hops:
                    last.append(len(plan) - 1)
        last = list(landed[0])
        for sign, hops in hops_of(sizes[second], False):
            for hop in range(1, hops + 1):
                block = [0, 0]
                block[second] = sign * (hops + 1 - hop)
                adds = list(landed[block[second] % sizes[second]])
                plan.append(
                    (second, sign, tuple(block), part, adds + ([] if hop == 1 else [len(plan) - 1]))
                )
            if hops:
                last.append(len(plan) - 1)
        ends[part] = last
    return plan, ends


def run_plan(plan, part_bytes, ready, add_time=0.0):
    cost = [part_bytes[message[3]] / LINK_RATE for message in plan]
    tail = list(cost)
    for index in reversed(range(len(plan))):
        for dep in plan[index][4]:
            tail[dep] = max(tail[dep], cost[dep] + HOP_TIME + tail[index])
    order = sorted(range(len(plan)), key=lambda index: -tail[index])
    free, arrival, events = {}, {}, []
    done, started, now = set(), set(), 0.0
    made = set()
    todo = list(ready)
    while len(done) < len(plan):
        for index in order:
            axis, sign, block, part, deps = plan[index]
            if index in started or any(dep not in done for dep in deps):
                continue
            if (ready and block[0] not in made) or free.get((axis, sign), 0.0) > now + BACKLOG:
                continue
            started.add(index)
            now += add_time if deps else 0.0
            free[axis, sign] = max(now, free.get((axis, sign), 0.0)) + cost[index]
            arrival[index] = free[axis, sign] + HOP_TIME
            events.append(("start", index))
        coming = sorted((when, index) for index, when in arrival.items() if index not in done)
        if todo and (not coming or coming[0][0] > now):
            step = todo.pop(0)
            events.append(("make", step))
            made.update(step)
            now += BLOCK_TIME
        else:
            when, index = coming[0]
            now = max(now, when)
            done.add(index)
            events.append(("wait", index))
    return events


def head_groups(heads):
    sizes = [1] + [2] * ((heads - 2) // 2) + [1] if heads > 2 else [1] * heads
    starts = [sum(sizes[:index]) for index in range(len(sizes))]
    return [(start * HDIM, size * HDIM) for start, size in zip(starts, sizes)]


def chain_kernel(
    x_ref, go_ref, gain_ref, gate_ref, shard_ref, kept_ref, links_ref,
    out_ref, grad_ref,
    w_ref, wgrad, slots_a, slots_b,
    keys, inv_s, mean_s, q_s, pt_s, kt_s, dy_buf, lr_send, lr_recv, kgo_s, ng_s, qg_s,
    own_sem, gsend, grecv, ssend, srecv,
    nsend, nrecv, lsend, lrecv, dsend, drecv,
):
    sections = lax.axis_size("section")
    tiles = lax.axis_size("seq")
    sec = lax.axis_index("section")
    seq = lax.axis_index("seq")
    fsdp = lax.axis_index("fsdp")
    rows, width = x_ref.shape
    heads = width // HDIM
    spans = head_groups(heads)
    groups = len(spans)
    scale = HDIM ** (-0.5)
    ring_z = lax.axis_size("fsdp")
    shard = width // (ring_z * tiles)
    cut = first_columns(width)
    columns = (pl.ds(0, cut), pl.ds(cut, width - cut))
    half = width // 256 * 128
    gather_columns = (pl.ds(0, half), pl.ds(half, width - half))
    part_bytes = (2 * shard * cut, 2 * shard * (width - cut))
    left_rows = rows // LEFT_PARTS
    gather_bytes = (2 * shard * half, 2 * shard * (width - half), 2 * left_rows * width)

    def neighbour(axis, sign):
        if axis == 0:
            return (sec, lax.rem(fsdp + sign + ring_z, ring_z), seq)
        return (sec, fsdp, lax.rem(seq + sign + tiles, tiles))

    def rows_of(block):
        at_z = lax.rem(fsdp + block[0] + ring_z, ring_z)
        at_y = lax.rem(seq + block[1] + tiles, tiles)
        return pl.ds(pl.multiple_of((at_z * tiles + at_y) * shard, shard), shard)

    barrier = pltpu.get_barrier_semaphore()
    for other in (
        (lax.rem(sec + 1, sections), fsdp, seq),
        (lax.rem(sec + sections - 1, sections), fsdp, seq),
        (sec, fsdp, lax.rem(seq + 1, tiles)),
        (sec, fsdp, lax.rem(seq + tiles - 1, tiles)),
        (sec, lax.rem(fsdp + 1, ring_z), seq),
        (sec, lax.rem(fsdp + ring_z - 1, ring_z), seq),
    ):
        pl.semaphore_signal(barrier, inc=1, device_id=other, device_id_type=MESH)

    own_copy = pltpu.make_async_copy(shard_ref, w_ref.at[rows_of((0, 0)), :], own_sem)
    own_copy.start()
    keep = kept_ref[0, sec]
    linked = links_ref[0, 0] * jnp.minimum(seq, 1)

    def norm_block(step, carry):
        at = pl.ds(pl.multiple_of(step * 16, 16), 16)
        x_rows = x_ref[at, :].astype(jnp.float32)
        inv = lax.rsqrt(jnp.mean(x_rows * x_rows, axis=-1, keepdims=True) + norm_eps)
        inv_s[at, :] = jnp.broadcast_to(inv, (16, HDIM))
        rounded = (x_rows * inv * gain_ref[...]).astype(jnp.bfloat16)
        keys[pl.ds(pl.multiple_of(rows + step * 16, 16), 16), :] = rounded
        return carry

    lax.fori_loop(0, rows // 16, norm_block, 0)

    @pl.when(seq == 0)
    def _():
        keys[0:rows, :] = jnp.zeros((rows, width), jnp.bfloat16)

    @pl.when(seq == tiles - 1)
    def _():
        lr_recv[...] = jnp.zeros_like(lr_recv)

    pl.semaphore_wait(barrier, 6)
    own_copy.wait()

    gather = spread_plan(ring_z, tiles)
    weight_count = len(gather)
    gather = gather + [(1, 1, (0, 0), 2, [])] * (LEFT_PARTS if tiles > 1 else 0)

    def gather_copy(index):
        axis, sign, block, part, _ = gather[index]
        if part == 2:
            step = (index - weight_count) * left_rows
            source = keys.at[pl.ds(rows + step, left_rows), :]
            place = keys.at[pl.ds(step, left_rows), :]
        else:
            source = place = w_ref.at[rows_of(block), gather_columns[part]]
        return pltpu.make_async_remote_copy(
            src_ref=source,
            dst_ref=place,
            send_sem=gsend.at[index],
            recv_sem=grecv.at[index],
            device_id=neighbour(axis, sign),
            device_id_type=MESH,
        )

    for kind, index in run_plan(gather, gather_bytes, ()):
        left = gather[index][3] == 2
        if kind == "start":
            if left:

                @pl.when(seq < tiles - 1)
                def _():
                    gather_copy(index).start()
            else:
                gather_copy(index).start()
            continue
        if left:

            @pl.when(seq > 0)
            def _():
                gather_copy(index).wait_recv()
        else:
            gather_copy(index).wait_recv()

    for start in range(0, width, GROUP):
        at = pl.ds(start, GROUP)
        q_s[:, at] = mm(keys[rows:, :], w_ref[:, at]).astype(jnp.bfloat16)

    position = lax.broadcasted_iota(jnp.int32, (2 * rows, rows), 0)
    valid = position + linked * rows >= rows
    for head in range(heads):
        at = pl.ds(head * HDIM, HDIM)
        key_part = keys[:, at]
        scores = mm(key_part, q_s[:, at], NT) * scale
        scores = jnp.where(valid, scores, -1e30)
        top = jnp.max(scores, axis=0, keepdims=True)
        weight = jnp.exp(scores - top)
        pt_s[head] = weight / jnp.sum(weight, axis=0, keepdims=True)
        kt_s[at, :] = key_part.T

    @pl.when(sec == sections - 1)
    def _():
        dy_buf[...] = go_ref[...]

    def dy_copy(group):
        at = pl.ds(*spans[group])
        return pltpu.make_async_remote_copy(
            src_ref=out_ref.at[:, at],
            dst_ref=dy_buf.at[:, at],
            send_sem=dsend.at[group],
            recv_sem=drecv.at[group],
            device_id=(lax.rem(sec + sections - 1, sections), fsdp, seq),
            device_id_type=MESH,
        )

    def lr_copy(group):
        at = pl.ds(*spans[group])
        return pltpu.make_async_remote_copy(
            src_ref=lr_send.at[:, at],
            dst_ref=lr_recv.at[:, at],
            send_sem=lsend.at[group],
            recv_sem=lrecv.at[group],
            device_id=(sec, fsdp, lax.rem(seq + tiles - 1, tiles)),
            device_id_type=MESH,
        )

    def attention(group):
        first, span = spans[group]
        for head in range(first // HDIM, (first + span) // HDIM):
            at = pl.ds(head * HDIM, HDIM)
            grad = (gate_ref[:, at] * dy_buf[:, at].astype(jnp.float32)).astype(jnp.bfloat16)
            probs = pt_s[head]
            prob_grad = mm(keys[:, at], grad, NT)
            delta = jnp.sum(probs * prob_grad, axis=0, keepdims=True)
            score_grad = (probs * (prob_grad - delta) * scale).astype(jnp.bfloat16)
            key_grad = mm(
                jnp.concatenate([score_grad, probs.astype(jnp.bfloat16)], axis=1),
                jnp.concatenate([q_s[:, at], grad], axis=0),
            )
            lr_send[:, at] = key_grad[:rows].astype(jnp.bfloat16)
            kgo_s[:, at] = key_grad[rows:]
            qg_s[:, at] = mm(kt_s[at, :], score_grad).astype(jnp.bfloat16).T

    def project(group):
        at = pl.ds(*spans[group])
        part = mm(qg_s[:, at], w_ref[:, at], NT)
        if group == 0:
            ng_s[...] = part
        else:
            ng_s[...] += part

    for group in range(groups):

        @pl.when(sec < sections - 1)
        def _():
            dy_copy(group).wait_recv()

        attention(group)

        @pl.when(seq > 0)
        def _():
            lr_copy(group).start()

        if group > 0:
            project(group - 1)
    project(groups - 1)

    last = pl.ds(*spans[-1])
    most = pl.ds(0, spans[-1][0])

    def finish():
        @pl.when(seq < tiles - 1)
        def _():
            for group in range(groups - 1):
                lr_copy(group).wait_recv()

        for start in range(0, rows, 16):
            at = pl.ds(start, 16)
            main = ng_s[at, most] + kgo_s[at, most] + lr_recv[at, most].astype(jnp.float32)
            main = main * gain_ref[:, most]
            ng_s[at, most] = main
            rest = (ng_s[at, last] + kgo_s[at, last]) * gain_ref[:, last]
            ng_s[at, last] = rest
            mean = jnp.sum(x_ref[at, most].astype(jnp.float32) * main, axis=-1, keepdims=True)
            mean = mean + jnp.sum(
                x_ref[at, last].astype(jnp.float32) * rest, axis=-1, keepdims=True
            )
            mean_s[at, :] = jnp.broadcast_to(mean, (16, HDIM))

        @pl.when(seq < tiles - 1)
        def _():
            lr_copy(groups - 1).wait_recv()

        added = lr_recv[:, last].astype(jnp.float32) * gain_ref[:, last]
        ng_s[:, last] += added
        mean = jnp.sum(x_ref[:, last].astype(jnp.float32) * added, axis=-1, keepdims=True)
        inv = inv_s[...]
        mean_s[...] = (mean_s[...] + mean) * (inv * inv * (1.0 / width))
        kept_here = jnp.full((rows, HDIM), keep, jnp.int32) > 0
        for group, (first, span) in enumerate(spans):
            for start in range(first, first + span, HDIM):
                at = pl.ds(start, HDIM)
                before = dy_buf[:, at].astype(jnp.float32)
                x_part = x_ref[:, at].astype(jnp.float32)
                change = inv_s[...] * (ng_s[:, at] - x_part * mean_s[...])
                out_ref[:, at] = jnp.where(kept_here, before + change, before).astype(
                    jnp.bfloat16
                )

            @pl.when(sec > 0)
            def _():
                dy_copy(group).start()

    @pl.when(sec > 0)
    def _():
        finish()

    grads = qg_s[...].astype(jnp.float32)
    qg_s[...] = jnp.where(
        jnp.full(grads.shape, keep, jnp.int32) > 0, grads, jnp.zeros_like(grads)
    ).astype(jnp.bfloat16)

    sums, ends = sum_plan(ring_z, tiles)
    slot_refs = (slots_a, slots_b)
    slot_at, used = {}, [0, 0]
    for index, (_, _, _, part, _) in enumerate(sums):
        slot_at[index] = used[part]
        used[part] += 1

    def sum_copy(index):
        axis, sign, block, part, _ = sums[index]
        return pltpu.make_async_remote_copy(
            src_ref=wgrad.at[rows_of(block), columns[part]],
            dst_ref=slot_refs[part].at[slot_at[index]],
            send_sem=ssend.at[index],
            recv_sem=srecv.at[index],
            device_id=neighbour(axis, sign),
            device_id_type=MESH,
        )

    def summed(block, part, adds):
        total = wgrad[rows_of(block), columns[part]].astype(jnp.float32)
        for index in adds:
            total = total + slot_refs[part][slot_at[index]].astype(jnp.float32)
        return total.astype(jnp.bfloat16)

    def make(offset):
        span = tiles * shard
        start = lax.rem(fsdp + offset + ring_z, ring_z) * span
        at = pl.ds(pl.multiple_of(start, shard), span)
        left = kt_s[at, rows : 2 * rows]
        for first in range(0, width, GROUP):
            to = pl.ds(first, GROUP)
            wgrad[at, to] = mm(left, qg_s[:, to]).astype(jnp.bfloat16)

    makes = []
    for offset in far_first(ring_z):
        makes.append((offset, offset - ring_z, offset + ring_z))
    unmade = len(makes)
    for kind, index in run_plan(sums, part_bytes, makes, 0.1):
        if kind == "make":
            make(index[0])
            unmade -= 1
        elif kind == "start":
            _, _, block, part, adds = sums[index]
            if adds:
                wgrad[rows_of(block), columns[part]] = summed(block, part, adds)
            sum_copy(index).start()
        else:
            if unmade == 0:
                unmade = -1

                @pl.when(sec == 0)
                def _():
                    finish()

            sum_copy(index).wait_recv()
    for index in range(len(gather)):
        if gather[index][3] != 2:
            gather_copy(index).wait_send()

    @pl.when(seq < tiles - 1)
    def _():
        for index in range(weight_count, len(gather)):
            gather_copy(index).wait_send()

    for part in (0, 1):
        grad_ref[:, columns[part]] = summed((0, 0), part, ends[part])
    for index in range(len(sums)):
        sum_copy(index).wait_send()

    @pl.when(seq > 0)
    def _():
        for group in range(groups):
            lr_copy(group).wait_send()

    @pl.when(sec > 0)
    def _():
        for group in range(groups):
            dy_copy(group).wait_send()


def first_columns(width):
    return max(1, round(width * 5 / 12 / 128)) * 128


def run_chain(x, grad_out, gain, gate, shard, kept, links):
    rows, width = x.shape
    heads = width // HDIM
    groups = len(head_groups(heads))
    vmem = pl.BlockSpec(memory_space=pltpu.VMEM)
    smem = pl.BlockSpec(memory_space=pltpu.SMEM)
    low = jnp.bfloat16
    count = lax.axis_size("fsdp") * lax.axis_size("seq") - 1
    cut = first_columns(width)
    dma = pltpu.SemaphoreType.DMA
    return pl.pallas_call(
        chain_kernel,
        out_shape=(
            jax.ShapeDtypeStruct((rows, width), low),
            jax.ShapeDtypeStruct(shard.shape, low),
        ),
        in_specs=[vmem] * 5 + [smem] * 2,
        out_specs=(vmem, vmem),
        scratch_shapes=[
            pltpu.VMEM((width, width), low),
            pltpu.VMEM((width, width), low),
            pltpu.VMEM((count, shard.shape[0], cut), low),
            pltpu.VMEM((count, shard.shape[0], width - cut), low),
            pltpu.VMEM((2 * rows, width), low),
            pltpu.VMEM((rows, HDIM), jnp.float32),
            pltpu.VMEM((rows, HDIM), jnp.float32),
            pltpu.VMEM((rows, width), low),
            pltpu.VMEM((heads, 2 * rows, rows), jnp.float32),
            pltpu.VMEM((width, 2 * rows), low),
            pltpu.VMEM((rows, width), low),
            pltpu.VMEM((rows, width), low),
            pltpu.VMEM((rows, width), low),
            pltpu.VMEM((rows, width), jnp.float32),
            pltpu.VMEM((rows, width), jnp.float32),
            pltpu.VMEM((rows, width), low),
            dma,
            dma((2 * count + LEFT_PARTS,)),
            dma((2 * count + LEFT_PARTS,)),
            dma((2 * count,)),
            dma((2 * count,)),
            dma,
            dma,
            dma((groups,)),
            dma((groups,)),
            dma((groups,)),
            dma((groups,)),
        ],
        compiler_params=pltpu.CompilerParams(
            collective_id=0, has_side_effects=True, vmem_limit_bytes=56 * 2**20
        ),
        name="chain",
    )(x, grad_out, gain, gate, shard, kept, links)


def per_device(acts, grad_out, gain, gate, w_query, kept, links):
    result, grad_rows = run_chain(
        acts[0, 0], grad_out[0], gain, gate, w_query[0], kept, links
    )
    return (result[None, None], grad_rows[None])


def solution(mesh):
    placed = (
        P("section", "fsdp", "seq", None),
        P("fsdp", "seq", None),
        P("section", None),
        P("section", None),
        P("section", ("fsdp", "seq"), None),
        P("fsdp", None),
        P("fsdp", "seq"),
    )
    return jax.shard_map(
        per_device,
        mesh=mesh,
        in_specs=placed,
        out_specs=(P("section", "fsdp", "seq", None), P("section", ("fsdp", "seq"), None)),
        check_vma=False,
    )
```
